32 devices in a mesh: groups: 2 (over x), seq: 16 (over z, y, core).
Axes of the slice: x: 2, y: 2, z: 4, core: 2. Of those that a mesh axis runs over, the one named last changes fastest.
Arguments:
- query_acts: bfloat16 [4096, 2048], P(('groups', 'seq')), parts along dimension 0, may hold values from -6 to 6
- key_acts: bfloat16 [4096, 2048], P(('groups', 'seq')), parts along dimension 0, may hold values from -6 to 6
- value_acts: bfloat16 [4096, 2048], P(('groups', 'seq')), parts along dimension 0, may hold values from -6 to 6
- beta_logit: float32 [16, 4096], P(None, ('groups', 'seq')), parts along dimension 1, may hold values from -9.3 to 3
- output_grad: bfloat16 [2048, 4096], P('seq', 'groups'), parts along dimension 1, may hold values from -6 to 6
- doc_lengths: int32 [8], P('groups'), parts along dimension 0, may hold values from 1 to 1024, 2048 in all
Outputs:
- query_grad: bfloat16 [2048, 4096], P('seq', 'groups'), parts along dimension 1
- key_grad: bfloat16 [4096, 2048], P(('groups', 'seq')), parts along dimension 0
- value_grad: bfloat16 [4096, 2048], P(('groups', 'seq')), parts along dimension 0
- beta_grad: float32 [16, 4096], P(None, ('groups', 'seq')), parts along dimension 1
The draws below stay inside these ranges and needn't reach their ends.
There are 2 independent parts, one for each index of `groups`. The reference program is written for one: setup_inputs(seed, part) draws one part's arguments, and reference() takes and returns one part's arrays. A program takes and returns all parts, laid end to end along the dimension named above; each array names one. Nothing has to cross between parts.
Inputs may be any that keep to these rules, and one draw needn't show every extreme that they name: `doc_lengths`: the 4 lengths sum to 2048, and the longest has exactly 1024 tokens.
All inputs are finite; a program needn't handle non-finite values.
Results may differ from the reference program's by a relative error of at most 0.001.
Values may be sent and summed in bfloat16 or wider, within the bound.
A program may use at most 192 MiB of HBM per device.

```python
import math
import jax
import jax.numpy as jnp
import numpy as np
from jax import lax

HEAD_SHARE = 16
HEAD_DIM = 128
BLOCK = 64
WIDTH = 2048
WINDOW_TOKENS = 2048
DOCS = 4
MOST_DOC = 1024


def draw_beta_logit(key, part):
    key_baseline, key_jagged, key_spike = jax.random.split(key, 3)
    slowest = 2.0 * HEAD_DIM / WINDOW_TOKENS
    fastest = 0.6
    spread = jax.random.uniform(key_baseline, (HEAD_SHARE, 1), jnp.float32)
    base_rate = jnp.exp(jnp.log(slowest) + spread * (jnp.log(fastest) - jnp.log(slowest)))
    roughness = jnp.exp(jax.random.uniform(key_jagged, (HEAD_SHARE, WINDOW_TOKENS), jnp.float32, -0.7, 0.7))
    intensity = base_rate * roughness
    spike_events = jax.random.uniform(key_spike, (HEAD_SHARE, WINDOW_TOKENS), jnp.float32) < 6.0 / WINDOW_TOKENS
    intensity = jnp.where(spike_events, 0.9, intensity)
    intensity = jnp.clip(intensity, 0.0001, 0.95)
    return (jnp.log(intensity) - jnp.log1p(-intensity)).astype(jnp.float32)


def steps_of(stream_key, extent, cuts, low, high):
    def one(dim, blocks):
        heights = jax.random.uniform(jax.random.fold_in(jax.random.fold_in(stream_key, 6), dim), (blocks,), jnp.float32, low / len(cuts), high / len(cuts))
        return jnp.repeat(jnp.exp(heights), extent[dim] // blocks).reshape((-1,) + (1,) * (len(extent) - dim - 1))

    gain = one(*cuts[0])
    for cut in cuts[1:]:
        gain = gain * one(*cut)
    return gain


def profile(count, total, reach, lean):
    weights = [(1 << 20) // math.isqrt(standing ** lean) + 1 for standing in range(2, count + 1)]
    spare, given = total - reach - (count - 1), [1] * (count - 1)
    while spare > 0:
        free = [i for i in range(count - 1) if given[i] < reach]
        whole, left = sum([weights[i] for i in free]), spare
        for i in free:
            extra = min(reach - given[i], max(1, left * weights[i] // whole), spare)
            given[i] = given[i] + extra
            spare = spare - extra
    return np.array([reach] + given)


def ragged_sizes(own_key, amount, total, reach, slope):
    if amount == 2:
        one = jax.random.randint(own_key, (), max(1, total - reach), min(reach, total - 1) + 1)
        return jnp.stack([one, total - one])
    tallies = jnp.asarray(profile(amount, total, reach, slope), jnp.int32)
    couples = (amount - 1) // 2
    donor, sink = tallies[1:1 + 2 * couples:2], tallies[2:2 + 2 * couples:2]
    slack = jnp.minimum(donor - 1, reach - sink)
    passed = jax.random.randint(jax.random.fold_in(own_key, 1), (couples,), 0, 1 << 20) % (slack + 1)
    tallies = tallies.at[1:1 + 2 * couples:2].set(donor - passed).at[2:2 + 2 * couples:2].set(sink + passed)
    return tallies[jax.random.permutation(jax.random.fold_in(own_key, 2), amount)]


def centred(own_key, shape, scale, most, shards=(), held_as=jnp.bfloat16):
    values = scale * jax.random.normal(own_key, shape, jnp.float32)
    if shards:
        values = values * steps_of(own_key, shape, shards, -0.22, 0.18)
    return jnp.clip(values, -most, most).astype(held_as)


def setup_inputs(seed: int = 0, part: int = 0) -> dict:
    keys = jax.random.split(jax.random.key(seed), 7)
    part_keys = jax.random.split(jax.random.fold_in(keys[6], part), 7)
    query_acts = centred(part_keys[0], (WINDOW_TOKENS, WIDTH), 1.0, 6.0, ((0, 16),))
    key_acts = centred(part_keys[1], (WINDOW_TOKENS, WIDTH), 1.0, 6.0, ((0, 16),))
    value_acts = centred(part_keys[2], (WINDOW_TOKENS, WIDTH), 1.0, 6.0, ((0, 16),))
    beta_logit = draw_beta_logit(jax.random.fold_in(jax.random.fold_in(keys[6], part), 71), part)
    output_grad = centred(part_keys[4], (WIDTH, WINDOW_TOKENS), 1.0, 6.0, ((0, 16),))
    doc_lengths = ragged_sizes(part_keys[5], DOCS, WINDOW_TOKENS, MOST_DOC, 2).astype(jnp.int32)
    return dict(query_acts=query_acts, key_acts=key_acts, value_acts=value_acts, beta_logit=beta_logit, output_grad=output_grad, doc_lengths=doc_lengths)


HIGHEST = lax.Precision.HIGHEST

def normalize(values):
    return values * lax.rsqrt(lax.optimization_barrier(jnp.sum(values * values, axis=-1, keepdims=True)) + 1e-06)

def count_ends(positions, doc_ends):
    return lax.optimization_barrier(jnp.sum((positions[:, None] >= doc_ends[None, :]).astype(jnp.int32), axis=1)).astype(jnp.int32)

def block_pass(state_in, queries, keys_norm, values, intensity, doc_ids, prev_docs):
    head_count, length, head_depth = keys_norm.shape
    value_width = values.shape[2]
    blocks = prev_docs.shape[0]
    block_size = length // blocks
    query_blocks = queries.reshape(head_count, blocks, block_size, head_depth)
    key_blocks = keys_norm.reshape(head_count, blocks, block_size, head_depth)
    value_blocks = values.reshape(head_count, blocks, block_size, value_width)
    strength_blocks = intensity.reshape(head_count, blocks, block_size)
    block_ids = doc_ids.reshape(blocks, block_size)
    same_doc = (block_ids[:, :, None] == block_ids[:, None, :]).astype(jnp.float32)
    carried = (block_ids == prev_docs[:, None]).astype(jnp.float32)
    ones_table = jnp.ones((block_size, block_size), jnp.float32)
    strict_lower = jnp.tril(ones_table, -1)
    causal = jnp.tril(ones_table, 0)
    identity = jnp.eye(block_size, dtype=jnp.float32)
    key_gram = jnp.einsum('hncd,hned->hnce', key_blocks, key_blocks, precision=HIGHEST)
    system = identity + strength_blocks[..., :, None] * key_gram * same_doc[None] * strict_lower
    diagonal = identity * strength_blocks[..., :, None]
    solved = lax.linalg.triangular_solve(system, diagonal, left_side=True, lower=True)
    scores = jnp.einsum('hncd,hned->hnce', query_blocks, key_blocks, precision=HIGHEST) * (same_doc * causal)[None]
    last_doc = same_doc[:, -1, :]
    keep_state = carried[:, -1]

    def advance(carried_state, inputs):
        solved_b, scores_b, query_b, key_b, value_b, carried_b, last_b, keep_b = inputs
        projected = jnp.einsum('hcd,hvd->hcv', key_b, carried_state, precision=HIGHEST)
        deltas = jnp.einsum('hts,hsv->htv', solved_b, value_b - carried_b[None, :, None] * projected, precision=HIGHEST)
        outputs = carried_b[None, :, None] * jnp.einsum('hcd,hvd->hcv', query_b, carried_state, precision=HIGHEST)
        outputs = outputs + jnp.einsum('hts,hsv->htv', scores_b, deltas, precision=HIGHEST)
        new_state = keep_b * carried_state + jnp.einsum('hsv,hsd->hvd', deltas * last_b[None, :, None], key_b, precision=HIGHEST)
        return (new_state, outputs)
    inputs = (jnp.moveaxis(solved, 1, 0), jnp.moveaxis(scores, 1, 0), jnp.moveaxis(query_blocks, 1, 0), jnp.moveaxis(key_blocks, 1, 0), jnp.moveaxis(value_blocks, 1, 0), carried, last_doc, keep_state)
    final_state, block_outs = lax.scan(advance, state_in, inputs)
    block_outs = jnp.moveaxis(block_outs, 0, 1).reshape(head_count, length, value_width)
    return (block_outs, final_state)

def reference(query_acts, key_acts, value_acts, beta_logit, output_grad, doc_lengths):
    token_count = query_acts.shape[0]
    head_count = beta_logit.shape[0]
    head_depth = query_acts.shape[1] // head_count
    doc_ends = jnp.cumsum(doc_lengths).astype(jnp.int32)
    positions = jnp.arange(token_count, dtype=jnp.int32)
    doc_ids = count_ends(positions, doc_ends)
    starts = (jnp.arange(token_count // BLOCK, dtype=jnp.int32) * BLOCK - 1).astype(jnp.int32)
    prev_docs = jnp.where(starts >= 0, count_ends(starts, doc_ends), -1).astype(jnp.int32)
    cotangent = output_grad.astype(jnp.float32).reshape(head_count, head_depth, token_count).transpose(0, 2, 1)

    def split_heads(values):
        return values.reshape(token_count, head_count, head_depth).transpose(1, 0, 2)

    def forward(query_f, key_f, value_f, logit_f):
        state_in = jnp.zeros((head_count, head_depth, head_depth), jnp.float32)
        outputs = block_pass(state_in, normalize(split_heads(query_f)), normalize(split_heads(key_f)), split_heads(value_f), jax.nn.sigmoid(logit_f), doc_ids, prev_docs)
        return outputs[0]
    primal = (query_acts.astype(jnp.float32), key_acts.astype(jnp.float32), value_acts.astype(jnp.float32), beta_logit)
    pullback = jax.vjp(forward, *primal)[1]
    grads = pullback(cotangent)
    query_grad = grads[0].T.astype(jnp.bfloat16)
    return (query_grad, grads[1].astype(jnp.bfloat16), grads[2].astype(jnp.bfloat16), grads[3])
```

```python
import functools
import jax
import jax.numpy as jnp
from jax import lax
from jax.experimental import pallas as pl
from jax.experimental.pallas import tpu as pltpu
from jax.sharding import PartitionSpec as P

BLOCK = 64
CHUNK = 128
GROUP = 4
F32 = jnp.float32
BF16 = jnp.bfloat16


def dot(left, right, dims):
    return lax.dot_general(left, right, ((dims[:1], dims[1:]), ((), ())), preferred_element_type=F32)


def split(values):
    high = values.astype(BF16)
    return high, (values - high.astype(F32)).astype(BF16)


def dot2l(left, exact, dims=(1, 0)):
    high, low = left
    return dot(high, exact, dims) + dot(low, exact, dims)


def dot2r(exact, right, dims=(1, 0)):
    high, low = right
    return dot(exact, high, dims) + dot(exact, low, dims)


def dot3(left, right, dims=(1, 0)):
    return dot(left[0], right[0], dims) + (dot(left[1], right[0], dims) + dot(left[0], right[1], dims))


def across(column):
    return jnp.broadcast_to(column, (CHUNK, CHUNK)).T


def inverse_norm(values):
    wide = values.astype(F32)
    return lax.rsqrt(jnp.sum(wide * wide, axis=1, keepdims=True) + 1e-06)


def doc_of(positions, ends):
    total = jnp.zeros(jnp.shape(positions), jnp.int32)
    for end in ends:
        total = total + (positions >= end).astype(jnp.int32)
    return total


def chunk_masks(index, ends):
    first = index * CHUNK
    down = first + lax.broadcasted_iota(jnp.int32, (CHUNK, CHUNK), 0)
    over = first + lax.broadcasted_iota(jnp.int32, (CHUNK, CHUNK), 1)
    doc_down = doc_of(down, ends)
    doc_over = doc_of(over, ends)
    before = jnp.where(first > 0, doc_of(first - 1, ends), -1)
    last = doc_of(first + CHUNK - 1, ends)
    same = doc_down == doc_over
    causal = jnp.where(same & (down >= over), 1.0, 0.0)
    strict = jnp.where(same & (down > over), 1.0, 0.0)
    carried = jnp.where(doc_down == before, 1.0, 0.0)
    closing = jnp.where(doc_down == last, 1.0, 0.0)
    keep = jnp.where(before == last, 1.0, 0.0)
    return causal, strict, carried, closing, keep


def invert(systems):
    rows = lax.broadcasted_iota(jnp.int32, (CHUNK, CHUNK), 0)
    cols = lax.broadcasted_iota(jnp.int32, (CHUNK, CHUNK), 1)
    eye = jnp.where(rows == cols, 1.0, 0.0)
    size = 1
    solved = None
    while size < CHUNK:
        pair = (rows // (2 * size) == cols // (2 * size)) & (rows // size != cols // size)
        corners = [jnp.where(pair, system, 0.0) for system in systems]
        if solved is None:
            solved = [eye - corner for corner in corners]
        else:
            parts = [split(value) for value in solved]
            inner = [dot3(split(corner), part) for corner, part in zip(corners, parts)]
            solved = [
                value - dot3(part, split(middle))
                for value, part, middle in zip(solved, parts, inner)
            ]
        size *= 2
    return solved


def ends_of(lengths_ref):
    ends = []
    total = 0
    for i in range(lengths_ref.shape[0]):
        total = total + lengths_ref[i]
        ends.append(total)
    return ends


def prepare(indices, ends, load, store):
    items = []
    for index in indices:
        query, key, value, cotangent, strength = load(index)
        causal, strict, carried, closing, keep = chunk_masks(index, ends)
        norm_q, norm_k = inverse_norm(query), inverse_norm(key)
        key_over = across(norm_k)
        gram = dot(key, key, (1, 1)) * norm_k * key_over
        scores = dot(query, key, (1, 1)) * norm_q * key_over * causal
        strength_down = strength.T
        items.append(
            (index, query, key, value, cotangent, carried, closing, keep, norm_q, norm_k,
             key_over, scores, strength, strength_down * gram * strict)
        )
    solved = invert([item[-1] for item in items])
    for item, inverse in zip(items, solved):
        (index, query, key, value, cotangent, carried, closing, keep, norm_q, norm_k,
         key_over, scores, strength, _) = item
        weighted = inverse * strength
        local = dot2l(split(weighted), value)
        response_k = dot2l(split(weighted * key_over * carried.T), key)
        ending = dot2l(split((weighted * (closing * norm_k)).T), key)
        offset = dot2r(value, split(ending), (0, 0))
        step = dot2r(key, split(ending * (carried * norm_k)), (0, 0))
        scores_parts = split(scores)
        response = carried * norm_q * query.astype(F32) - dot3(scores_parts, split(response_k))
        seed = dot2r(cotangent, split(response))
        early = dot2l(split(scores.T), cotangent, (1, 1))
        store(index, inverse, scores, local, response_k, offset, step, seed, early)


def finish(index, ends, load, stored, state, adjoint):
    query, key, value, cotangent, strength = load(index)
    inverse, scores, local, response_k, early = stored
    causal, strict, carried, closing, keep = chunk_masks(index, ends)
    norm_q, norm_k = inverse_norm(query), inverse_norm(key)
    key_f = key.astype(F32) * norm_k
    query_f = query.astype(F32) * norm_q
    key_over = across(norm_k)
    query_over = across(norm_q)
    strength_down = strength.T
    state_parts = split(state)
    adjoint_parts = split(adjoint)
    turned = cotangent.astype(F32).T.astype(BF16)
    deltas = local - dot3(split(response_k), state_parts, (1, 1))
    delta_parts = split(deltas)
    delta_grad = early + closing * norm_k * dot2r(key, adjoint_parts, (1, 1))
    right_grad = dot3(split(inverse.T), split(delta_grad))
    value_grad = strength_down * right_grad
    logit_grad = (1.0 - strength_down) * jnp.sum(right_grad * deltas, axis=1, keepdims=True)
    system_grad = -strength_down * strict * dot3(split(right_grad), delta_parts, (1, 1))
    scores_grad = causal * dot2r(turned, delta_parts, (1, 1))
    gram_grad = system_grad + system_grad.T
    query_norm_grad = dot2l(split(scores_grad * key_over), key)
    query_norm_grad = query_norm_grad + carried * dot2r(turned, state_parts)
    key_norm_grad = dot2l(split(gram_grad * key_over), key)
    key_norm_grad = key_norm_grad + dot2l(split(scores_grad.T * query_over), query)
    key_norm_grad = key_norm_grad + dot3(split(closing * deltas), adjoint_parts)
    key_norm_grad = key_norm_grad - dot3(split(carried * value_grad), state_parts)
    query_grad = norm_q * (
        query_norm_grad - query_f * jnp.sum(query_f * query_norm_grad, axis=1, keepdims=True)
    )
    key_grad = norm_k * (
        key_norm_grad - key_f * jnp.sum(key_f * key_norm_grad, axis=1, keepdims=True)
    )
    return query_grad.T.astype(BF16), key_grad.astype(BF16), value_grad.astype(BF16), across(logit_grad)[:1]


def head_kernel(
    lengths_ref, query_ref, key_ref, value_ref, logit_ref, cotangent_ref,
    query_out, key_out, value_out, logit_out,
    inverse_ref, scores_ref, local_ref, response_ref, offset_ref, step_ref, seed_ref, early_ref,
    state_ref, adjoint_ref,
):
    chunks = query_ref.shape[0]
    ends = ends_of(lengths_ref)

    def load(index):
        logit = jnp.broadcast_to(logit_ref[index], (CHUNK, CHUNK))
        strength = 1.0 / (1.0 + jnp.exp(-logit))
        return query_ref[index], key_ref[index], value_ref[index], cotangent_ref[index], strength

    def store(index, inverse, scores, local, response_k, offset, step, seed, early):
        inverse_ref[index] = inverse
        scores_ref[index] = scores
        local_ref[index] = local
        response_ref[index] = response_k
        offset_ref[index] = offset
        step_ref[index] = step
        seed_ref[index] = seed
        early_ref[index] = early

    def early_body(turn, carry):
        prepare([turn * GROUP + i for i in range(GROUP)], ends, load, store)
        return carry

    lax.fori_loop(0, chunks // GROUP, early_body, 0)

    def keep_of(index):
        first = index * CHUNK
        before = jnp.where(first > 0, doc_of(first - 1, ends), -1)
        return jnp.where(before == doc_of(first + CHUNK - 1, ends), 1.0, 0.0)

    def chain(turn, carry):
        state, adjoint = carry
        back = chunks - 1 - turn
        state_ref[turn] = state
        adjoint_ref[back] = adjoint
        moved = dot3(split(state), split(step_ref[turn]))
        pulled = dot3(split(adjoint), split(step_ref[back]), (1, 1))
        state = keep_of(turn) * state - moved + offset_ref[turn]
        adjoint = keep_of(back) * adjoint - pulled + seed_ref[back]
        return state, adjoint

    zero = jnp.zeros((CHUNK, CHUNK), F32)
    lax.fori_loop(0, chunks, chain, (zero, zero))

    def late_body(turn, carry):
        for i in range(2):
            index = turn * 2 + i
            stored = (inverse_ref[index], scores_ref[index], local_ref[index],
                      response_ref[index], early_ref[index])
            results = finish(index, ends, load, stored, state_ref[index], adjoint_ref[index])
            query_out[index] = results[0]
            key_out[index] = results[1]
            value_out[index] = results[2]
            logit_out[index] = results[3]
        return carry

    lax.fori_loop(0, chunks // 2, late_body, 0)


def head_pass(query, key, value, logit, cotangent, lengths, interpret=False):
    chunks = query.shape[0]
    square = (chunks, CHUNK, CHUNK)
    whole = pl.BlockSpec(memory_space=pltpu.VMEM)
    return pl.pallas_call(
        head_kernel,
        in_specs=[pl.BlockSpec(memory_space=pltpu.SMEM)] + [whole] * 5,
        out_specs=[whole] * 4,
        out_shape=[jax.ShapeDtypeStruct(square, BF16)] * 3
        + [jax.ShapeDtypeStruct((chunks, 1, CHUNK), F32)],
        scratch_shapes=[pltpu.VMEM(square, F32)] * 10,
        compiler_params=pltpu.CompilerParams(vmem_limit_bytes=48 << 20),
        interpret=interpret,
    )(lengths, query, key, value, logit, cotangent)


HIGHEST = lax.Precision.HIGHEST


def from_partner(block, axis, bit):
    count = lax.axis_size(axis)
    route = []
    for low in range(count):
        high = low | 1 << bit
        if high != low and high < count:
            route += [(low, high), (high, low)]
    return lax.ppermute(block, axis, route)


def normalize(values):
    return values * lax.rsqrt(jnp.sum(values * values, axis=-1, keepdims=True) + 1e-06)


def count_ends(positions, doc_ends):
    return jnp.sum((positions[:, None] >= doc_ends[None, :]).astype(jnp.int32), axis=1)


def matmul(left, right):
    return jnp.einsum("hij,hjk->hik", left, right, precision=HIGHEST)


def times_transposed(left, right):
    return jnp.einsum("hij,hkj->hik", left, right, precision=HIGHEST)


def block_pass(state_in, queries, keys_norm, values, intensity, doc_ids, prev_docs):
    head_count, length, head_depth = keys_norm.shape
    value_width = values.shape[2]
    blocks = prev_docs.shape[0]
    block_size = length // blocks
    query_blocks = queries.reshape(head_count, blocks, block_size, head_depth)
    key_blocks = keys_norm.reshape(head_count, blocks, block_size, head_depth)
    value_blocks = values.reshape(head_count, blocks, block_size, value_width)
    strength_blocks = intensity.reshape(head_count, blocks, block_size)
    block_ids = doc_ids.reshape(blocks, block_size)
    same_doc = (block_ids[:, :, None] == block_ids[:, None, :]).astype(jnp.float32)
    carried = (block_ids == prev_docs[:, None]).astype(jnp.float32)
    ones_table = jnp.ones((block_size, block_size), jnp.float32)
    strict_lower = jnp.tril(ones_table, -1)
    causal = jnp.tril(ones_table, 0)
    identity = jnp.eye(block_size, dtype=jnp.float32)
    key_gram = jnp.einsum("hncd,hned->hnce", key_blocks, key_blocks, precision=HIGHEST)
    system = identity + strength_blocks[..., :, None] * key_gram * same_doc[None] * strict_lower
    diagonal = identity * strength_blocks[..., :, None]
    solved = lax.linalg.triangular_solve(system, diagonal, left_side=True, lower=True)
    scores = (
        jnp.einsum("hncd,hned->hnce", query_blocks, key_blocks, precision=HIGHEST)
        * (same_doc * causal)[None]
    )
    last_doc = same_doc[:, -1, :]
    keep_state = carried[:, -1]

    def advance(carried_state, inputs):
        solved_b, scores_b, query_b, key_b, value_b, carried_b, last_b, keep_b = inputs
        projected = jnp.einsum("hcd,hvd->hcv", key_b, carried_state, precision=HIGHEST)
        deltas = jnp.einsum(
            "hts,hsv->htv",
            solved_b,
            value_b - carried_b[None, :, None] * projected,
            precision=HIGHEST,
        )
        outputs = carried_b[None, :, None] * jnp.einsum(
            "hcd,hvd->hcv", query_b, carried_state, precision=HIGHEST
        )
        outputs = outputs + jnp.einsum("hts,hsv->htv", scores_b, deltas, precision=HIGHEST)
        new_state = keep_b * carried_state + jnp.einsum(
            "hsv,hsd->hvd", deltas * last_b[None, :, None], key_b, precision=HIGHEST
        )
        return (new_state, outputs)

    inputs = (
        jnp.moveaxis(solved, 1, 0),
        jnp.moveaxis(scores, 1, 0),
        jnp.moveaxis(query_blocks, 1, 0),
        jnp.moveaxis(key_blocks, 1, 0),
        jnp.moveaxis(value_blocks, 1, 0),
        carried,
        last_doc,
        keep_state,
    )
    final_state, block_outs = lax.scan(advance, state_in, inputs)
    block_outs = jnp.moveaxis(block_outs, 0, 1).reshape(head_count, length, value_width)
    return (block_outs, final_state)


def butterfly(transfer, offset, adjoint_seed, identity, zero_state, shard_index, devices):
    totals = (transfer, offset, adjoint_seed)
    prefix = (identity, zero_state)
    suffix = (identity, zero_state)
    for bit_level in range(devices.bit_length() - 1):
        partner = from_partner(totals, "seq", bit_level)
        is_upper = shard_index // 2**bit_level % 2

        def from_lower(operand):
            new_prefix = (matmul(partner[0], prefix[0]), matmul(partner[1], prefix[0]) + prefix[1])
            new_totals = (
                matmul(partner[0], totals[0]),
                matmul(partner[1], totals[0]) + totals[1],
                times_transposed(totals[2], partner[0]) + partner[2],
            )
            return (new_prefix, suffix, new_totals)

        def from_upper(operand):
            new_suffix = (
                matmul(suffix[0], partner[0]),
                times_transposed(partner[2], suffix[0]) + suffix[1],
            )
            new_totals = (
                matmul(totals[0], partner[0]),
                matmul(totals[1], partner[0]) + partner[1],
                times_transposed(partner[2], totals[0]) + totals[2],
            )
            return (prefix, new_suffix, new_totals)

        prefix, suffix, totals = lax.cond(is_upper == 1, from_lower, from_upper, 0)
    return (prefix[1], suffix[1])


def shards_by_tokens(query_acts, key_acts, value_acts, beta_logit, output_grad, doc_lengths):
    devices = lax.axis_size("seq")
    shard_index = lax.axis_index("seq")
    length = query_acts.shape[0]
    head_count = beta_logit.shape[0]
    feature_width = query_acts.shape[1]
    head_depth = feature_width // head_count
    blocks = length // BLOCK
    gathered = lax.all_to_all(output_grad, "seq", split_axis=1, concat_axis=0, tiled=True)
    cotangent = (
        gathered.astype(jnp.float32).reshape(head_count, head_depth, length).transpose(0, 2, 1)
    )
    doc_ends = jnp.cumsum(doc_lengths)
    first_token = shard_index * length
    positions = first_token + jnp.arange(length, dtype=jnp.int32)
    doc_ids = count_ends(positions, doc_ends)
    starts = first_token + jnp.arange(blocks, dtype=jnp.int32) * BLOCK - 1
    prev_docs = jnp.where(starts >= 0, count_ends(starts, doc_ends), -1)

    def split_heads(values):
        return values.reshape(length, head_count, head_depth).transpose(1, 0, 2)

    query_f = query_acts.astype(jnp.float32)
    key_f = key_acts.astype(jnp.float32)
    value_f = value_acts.astype(jnp.float32)
    query_norm = normalize(split_heads(query_f))
    key_norm = normalize(split_heads(key_f))
    value_heads = split_heads(value_f)
    intensity = jax.nn.sigmoid(beta_logit)
    identity = jnp.broadcast_to(
        jnp.eye(head_depth, dtype=jnp.float32), (head_count, head_depth, head_depth)
    )
    zero_state = jnp.zeros((head_count, head_depth, head_depth), jnp.float32)
    lifted_state = jnp.concatenate([identity, zero_state], axis=1)
    lifted_values = jnp.concatenate([jnp.zeros_like(value_heads), value_heads], axis=2)
    lifted_out, lifted_end = block_pass(
        lifted_state, query_norm, key_norm, lifted_values, intensity, doc_ids, prev_docs
    )
    transfer = lifted_end[:, :head_depth]
    offset = lifted_end[:, head_depth:]
    response = lifted_out[..., :head_depth]
    adjoint_seed = jnp.einsum("htv,htd->hvd", cotangent, response, precision=HIGHEST)
    state_in, grad_out = butterfly(
        transfer, offset, adjoint_seed, identity, zero_state, shard_index, devices
    )

    def forward(query_in, key_in, value_in, logit_in):
        return block_pass(
            state_in,
            normalize(split_heads(query_in)),
            normalize(split_heads(key_in)),
            split_heads(value_in),
            jax.nn.sigmoid(logit_in),
            doc_ids,
            prev_docs,
        )

    pullback = jax.vjp(forward, query_f, key_f, value_f, beta_logit)[1]
    grads = pullback((cotangent, grad_out))
    query_local = grads[0].T.astype(jnp.bfloat16)
    query_grad = lax.all_to_all(query_local, "seq", split_axis=0, concat_axis=1, tiled=True)
    return (query_grad, grads[1].astype(jnp.bfloat16), grads[2].astype(jnp.bfloat16), grads[3])


def shards(query_acts, key_acts, value_acts, beta_logit, output_grad, doc_lengths):
    devices = lax.axis_size("seq")
    length, width = query_acts.shape
    head_count = beta_logit.shape[0]
    window = length * devices
    chunks = window // CHUNK
    by_heads = devices == head_count and width == head_count * CHUNK and chunks % GROUP == 0
    if not by_heads or window % CHUNK:
        return shards_by_tokens(
            query_acts, key_acts, value_acts, beta_logit, output_grad, doc_lengths
        )

    def to_heads(values):
        moved = lax.all_to_all(values, "seq", split_axis=1, concat_axis=0, tiled=True)
        return moved.reshape(chunks, CHUNK, CHUNK)

    def to_tokens(values):
        return lax.all_to_all(
            values.reshape(window, CHUNK), "seq", split_axis=0, concat_axis=1, tiled=True
        )

    logit = lax.all_to_all(beta_logit, "seq", split_axis=0, concat_axis=1, tiled=True)
    cotangent = output_grad.reshape(CHUNK, chunks, CHUNK).transpose(1, 0, 2)
    grads = head_pass(
        to_heads(query_acts),
        to_heads(key_acts),
        to_heads(value_acts),
        logit.reshape(chunks, 1, CHUNK),
        cotangent,
        doc_lengths,
    )
    query_grad = grads[0].transpose(1, 0, 2).reshape(CHUNK, window)
    logit_grad = lax.all_to_all(
        grads[3].reshape(1, window), "seq", split_axis=1, concat_axis=0, tiled=True
    )
    return query_grad, to_tokens(grads[1]), to_tokens(grads[2]), logit_grad


def solution(mesh):
    placed = (
        P(("groups", "seq"), None),
        P(("groups", "seq"), None),
        P(("groups", "seq"), None),
        P(None, ("groups", "seq")),
        P("seq", "groups"),
        P("groups"),
    )
    return jax.shard_map(
        shards,
        mesh=mesh,
        in_specs=placed,
        out_specs=(
            P("seq", "groups"),
            P(("groups", "seq"), None),
            P(("groups", "seq"), None),
            P(None, ("groups", "seq")),
        ),
        check_vma=False,
    )
```

```python
import functools
import jax
import jax.numpy as jnp
from jax import lax
from jax.experimental import pallas as pl
from jax.experimental.pallas import tpu as pltpu
from jax.sharding import PartitionSpec as P

BLOCK = 64
CHUNK = 128
GROUP = 4
LATE = 2
F32 = jnp.float32
BF16 = jnp.bfloat16


def dot(left, right, dims):
    return lax.dot_general(left, right, ((dims[:1], dims[1:]), ((), ())), preferred_element_type=F32)


def split(values):
    high = values.astype(BF16)
    return high, (values - high.astype(F32)).astype(BF16)


def dot2l(left, exact, dims=(1, 0)):
    high, low = left
    return dot(high, exact, dims) + dot(low, exact, dims)


def dot2r(exact, right, dims=(1, 0)):
    high, low = right
    return dot(exact, high, dims) + dot(exact, low, dims)


def dot3(left, right, dims=(1, 0)):
    return dot(left[0], right[0], dims) + (dot(left[1], right[0], dims) + dot(left[0], right[1], dims))


def across(column):
    return jnp.broadcast_to(column, (CHUNK, CHUNK)).T


def inverse_norm(values):
    wide = values.astype(F32)
    return lax.rsqrt(jnp.sum(wide * wide, axis=1, keepdims=True) + 1e-06)


def doc_of(positions, ends):
    total = jnp.zeros(jnp.shape(positions), jnp.int32)
    for end in ends:
        total = total + (positions >= end).astype(jnp.int32)
    return total


def chunk_masks(index, ends):
    first = index * CHUNK
    down = first + lax.broadcasted_iota(jnp.int32, (CHUNK, CHUNK), 0)
    over = first + lax.broadcasted_iota(jnp.int32, (CHUNK, CHUNK), 1)
    doc_down = doc_of(down, ends)
    doc_over = doc_of(over, ends)
    before = jnp.where(first > 0, doc_of(first - 1, ends), -1)
    last = doc_of(first + CHUNK - 1, ends)
    same = doc_down == doc_over
    causal = jnp.where(same & (down >= over), 1.0, 0.0)
    strict = jnp.where(same & (down > over), 1.0, 0.0)
    carried = jnp.where(doc_down == before, 1.0, 0.0)
    closing = jnp.where(doc_down == last, 1.0, 0.0)
    keep = jnp.where(before == last, 1.0, 0.0)
    return causal, strict, carried, closing, keep


def invert(systems):
    rows = lax.broadcasted_iota(jnp.int32, (CHUNK, CHUNK), 0)
    cols = lax.broadcasted_iota(jnp.int32, (CHUNK, CHUNK), 1)
    eye = jnp.where(rows == cols, 1.0, 0.0)
    size = 1
    solved = None
    while size < CHUNK:
        pair = (rows // (2 * size) == cols // (2 * size)) & (rows // size != cols // size)
        corners = [jnp.where(pair, system, 0.0) for system in systems]
        if solved is None:
            solved = [eye - corner for corner in corners]
        else:
            parts = [split(value) for value in solved]
            inner = [dot3(split(corner), part) for corner, part in zip(corners, parts)]
            solved = [
                value - dot3(part, split(middle))
                for value, part, middle in zip(solved, parts, inner)
            ]
        size *= 2
    return solved


def ends_of(lengths_ref):
    ends = []
    total = 0
    for i in range(lengths_ref.shape[0]):
        total = total + lengths_ref[i]
        ends.append(total)
    return ends


def prepare(indices, ends, load, store):
    items = []
    for index in indices:
        query, key, value, cotangent, strength = load(index)
        causal, strict, carried, closing, keep = chunk_masks(index, ends)
        norm_q, norm_k = inverse_norm(query), inverse_norm(key)
        key_over = across(norm_k)
        gram = dot(key, key, (1, 1)) * norm_k * key_over
        scores = dot(query, key, (1, 1)) * norm_q * key_over * causal
        strength_down = strength.T
        items.append(
            (index, query, key, value, cotangent, carried, closing, keep, norm_q, norm_k,
             key_over, scores, strength, strength_down * gram * strict)
        )
    solved = invert([item[-1] for item in items])
    for item, inverse in zip(items, solved):
        (index, query, key, value, cotangent, carried, closing, keep, norm_q, norm_k,
         key_over, scores, strength, _) = item
        weighted = inverse * strength
        local = dot2l(split(weighted), value)
        response_k = dot2l(split(weighted * key_over * carried.T), key)
        ending = dot2l(split((weighted * (closing * norm_k)).T), key)
        offset = dot2r(value, split(ending), (0, 0))
        step = dot2r(key, split(ending * (carried * norm_k)), (0, 0))
        scores_parts = split(scores)
        response = carried * norm_q * query.astype(F32) - dot3(scores_parts, split(response_k))
        seed = dot2r(cotangent, split(response))
        early = dot2l(split(scores.T), cotangent, (1, 1))
        store(index, inverse, scores, local, response_k, offset, step, seed, early)


def finish(index, ends, load, stored, state, adjoint):
    query, key, value, cotangent, strength = load(index)
    inverse, scores, local, response_k, early = stored
    causal, strict, carried, closing, keep = chunk_masks(index, ends)
    norm_q, norm_k = inverse_norm(query), inverse_norm(key)
    key_f = key.astype(F32) * norm_k
    query_f = query.astype(F32) * norm_q
    key_over = across(norm_k)
    query_over = across(norm_q)
    strength_down = strength.T
    state_parts = split(state)
    adjoint_parts = split(adjoint)
    turned = cotangent.astype(F32).T.astype(BF16)
    deltas = local - dot3(split(response_k), state_parts, (1, 1))
    delta_parts = split(deltas)
    delta_grad = early + closing * norm_k * dot2r(key, adjoint_parts, (1, 1))
    right_grad = dot3(split(inverse.T), split(delta_grad))
    value_grad = strength_down * right_grad
    logit_grad = (1.0 - strength_down) * jnp.sum(right_grad * deltas, axis=1, keepdims=True)
    system_grad = -strength_down * strict * dot3(split(right_grad), delta_parts, (1, 1))
    scores_grad = causal * dot2r(turned, delta_parts, (1, 1))
    gram_grad = system_grad + system_grad.T
    query_norm_grad = dot2l(split(scores_grad * key_over), key)
    query_norm_grad = query_norm_grad + carried * dot2r(turned, state_parts)
    key_norm_grad = dot2l(split(gram_grad * key_over), key)
    key_norm_grad = key_norm_grad + dot2l(split(scores_grad.T * query_over), query)
    key_norm_grad = key_norm_grad + dot3(split(closing * deltas), adjoint_parts)
    key_norm_grad = key_norm_grad - dot3(split(carried * value_grad), state_parts)
    query_grad = norm_q * (
        query_norm_grad - query_f * jnp.sum(query_f * query_norm_grad, axis=1, keepdims=True)
    )
    key_grad = norm_k * (
        key_norm_grad - key_f * jnp.sum(key_f * key_norm_grad, axis=1, keepdims=True)
    )
    return query_grad.T.astype(BF16), key_grad.astype(BF16), value_grad.astype(BF16), across(logit_grad)[:1]


def head_kernel(
    lengths_ref, query_ref, key_ref, value_ref, logit_ref, cotangent_ref,
    query_out, key_out, value_out, logit_out,
    query_in, key_in, value_in, logit_in, key_back, value_back, logit_back,
    inverse_ref, scores_ref, local_ref, response_ref, offset_ref, step_ref, seed_ref, early_ref,
    state_ref, adjoint_ref, in_send, in_recv, out_send, out_recv,
):
    chunks = key_in.shape[0]
    me = lax.axis_index("seq")
    ends = ends_of(lengths_ref)

    def columns(index):
        return pl.ds(pl.multiple_of(index * CHUNK, CHUNK), CHUNK)

    def ahead(offset):
        return lax.rem(me + offset, chunks)

    def in_pairs(owner, source):
        return [
            (key_ref.at[:, columns(owner)], key_in.at[source]),
            (value_ref.at[:, columns(owner)], value_in.at[source]),
            (query_ref.at[:, columns(owner)], query_in.at[source]),
            (logit_ref.at[owner], logit_in.at[source]),
        ]

    def out_pairs(index, head):
        return [
            (key_back.at[index], key_out.at[:, columns(head)]),
            (value_back.at[index], value_out.at[:, columns(head)]),
            (logit_back.at[index], logit_out.at[head]),
        ]

    def remote(pairs, send, recv, send_at, recv_at, peer):
        return [
            pltpu.make_async_remote_copy(
                src_ref=pair[0],
                dst_ref=pair[1],
                send_sem=send.at[i, send_at],
                recv_sem=recv.at[i, recv_at],
                device_id={"seq": peer},
                device_id_type=pl.DeviceIdType.MESH,
            )
            for i, pair in enumerate(pairs)
        ]

    def local_copies(pairs, sems):
        return [
            pltpu.make_async_copy(pair[0], pair[1], sems.at[i, me])
            for i, pair in enumerate(pairs)
        ]

    barrier = pltpu.get_barrier_semaphore()

    def greet(offset, carry):
        pl.semaphore_signal(
            barrier, inc=1, device_id={"seq": ahead(offset)}, device_id_type=pl.DeviceIdType.MESH
        )
        return carry

    own = local_copies(in_pairs(me, me), in_recv)
    for copy in own:
        copy.start()
    lax.fori_loop(1, chunks, greet, 0)
    pl.semaphore_wait(barrier, chunks - 1)

    def send(offset, carry):
        peer = ahead(offset)
        for copy in remote(in_pairs(peer, me), in_send, in_recv, peer, me, peer):
            copy.start()
        return carry

    lax.fori_loop(1, chunks, send, 0)
    for copy in own:
        copy.wait()

    def load(index):
        logit = jnp.broadcast_to(logit_in[index], (CHUNK, CHUNK))
        strength = 1.0 / (1.0 + jnp.exp(-logit))
        return (query_in[index], key_in[index], value_in[index],
                cotangent_ref[:, columns(index)], strength)

    def store(index, inverse, scores, local, response_k, offset, step, seed, early):
        inverse_ref[index] = inverse
        scores_ref[index] = scores
        local_ref[index] = local
        response_ref[index] = response_k
        offset_ref[index] = offset
        step_ref[index] = step
        seed_ref[index] = seed
        early_ref[index] = early

    def arrive(source):
        for copy in remote(in_pairs(me, source), in_send, in_recv, source, source, source):
            copy.wait_recv()

    def early_body(turn, carry):
        sources = [ahead(chunks - turn * GROUP - i) for i in range(GROUP)]

        @pl.when(turn > 0)
        def _():
            arrive(sources[0])

        for source in sources[1:]:
            arrive(source)
        prepare(sources, ends, load, store)
        return carry

    lax.fori_loop(0, chunks // GROUP, early_body, 0)

    def keep_of(index):
        first = index * CHUNK
        before = jnp.where(first > 0, doc_of(first - 1, ends), -1)
        return jnp.where(before == doc_of(first + CHUNK - 1, ends), 1.0, 0.0)

    def chain(turn, carry):
        state, adjoint = carry
        back = chunks - 1 - turn
        state_ref[turn] = state
        adjoint_ref[back] = adjoint
        moved = dot3(split(state), split(step_ref[turn]))
        pulled = dot3(split(adjoint), split(step_ref[back]), (1, 1))
        state = keep_of(turn) * state - moved + offset_ref[turn]
        adjoint = keep_of(back) * adjoint - pulled + seed_ref[back]
        return state, adjoint

    zero = jnp.zeros((CHUNK, CHUNK), F32)
    lax.fori_loop(0, chunks, chain, (zero, zero))

    def late_body(turn, carry):
        indices = [ahead(4 + turn * LATE + i) for i in range(LATE)]
        for index in indices:
            stored = (inverse_ref[index], scores_ref[index], local_ref[index],
                      response_ref[index], early_ref[index])
            results = finish(index, ends, load, stored, state_ref[index], adjoint_ref[index])
            query_out[:, columns(index)] = results[0]
            key_back[index] = results[1]
            value_back[index] = results[2]
            logit_back[index] = results[3]

        @pl.when(turn != (chunks - 4) // LATE)
        def _():
            for copy in remote(
                out_pairs(indices[0], me), out_send, out_recv, indices[0], me, indices[0]
            ):
                copy.start()

        @pl.when(turn == (chunks - 4) // LATE)
        def _():
            for copy in local_copies(out_pairs(me, me), out_recv):
                copy.start()

        for index in indices[1:]:
            for copy in remote(out_pairs(index, me), out_send, out_recv, index, me, index):
                copy.start()
        return carry

    lax.fori_loop(0, chunks // LATE, late_body, 0)

    for copy in local_copies(out_pairs(me, me), out_recv):
        copy.wait()

    def settle(offset, carry):
        peer = ahead(offset)
        for copy in remote(in_pairs(peer, me), in_send, in_recv, peer, me, peer):
            copy.wait_send()
        for copy in remote(out_pairs(peer, me), out_send, out_recv, peer, me, peer):
            copy.wait_send()
        for copy in remote(out_pairs(me, peer), out_send, out_recv, peer, peer, peer):
            copy.wait_recv()
        return carry

    lax.fori_loop(1, chunks, settle, 0)


def head_pass(query, key, value, logit, cotangent, lengths):
    length, width = query.shape
    heads = logit.shape[0]
    blocks = (heads, CHUNK, CHUNK)
    rows = (heads, 1, CHUNK)
    whole = pl.BlockSpec(memory_space=pltpu.VMEM)
    anywhere = pl.BlockSpec(memory_space=pl.ANY)
    return pl.pallas_call(
        head_kernel,
        in_specs=[pl.BlockSpec(memory_space=pltpu.SMEM), anywhere, anywhere, anywhere, whole, whole],
        out_specs=[whole, anywhere, anywhere, whole],
        out_shape=[
            jax.ShapeDtypeStruct((CHUNK, width), BF16),
            jax.ShapeDtypeStruct((length, width), BF16),
            jax.ShapeDtypeStruct((length, width), BF16),
            jax.ShapeDtypeStruct(rows, F32),
        ],
        scratch_shapes=[pltpu.VMEM(blocks, BF16)] * 3
        + [pltpu.VMEM(rows, F32)]
        + [pltpu.VMEM(blocks, BF16)] * 2
        + [pltpu.VMEM(rows, F32)]
        + [pltpu.VMEM(blocks, F32)] * 10
        + [pltpu.SemaphoreType.DMA((4, heads))] * 2
        + [pltpu.SemaphoreType.DMA((3, heads))] * 2,
        compiler_params=pltpu.CompilerParams(
            vmem_limit_bytes=48 << 20, collective_id=0, has_side_effects=True
        ),
    )(lengths, query, key, value, logit, cotangent)


HIGHEST = lax.Precision.HIGHEST


def from_partner(block, axis, bit):
    count = lax.axis_size(axis)
    route = []
    for low in range(count):
        high = low | 1 << bit
        if high != low and high < count:
            route += [(low, high), (high, low)]
    return lax.ppermute(block, axis, route)


def normalize(values):
    return values * lax.rsqrt(jnp.sum(values * values, axis=-1, keepdims=True) + 1e-06)


def count_ends(positions, doc_ends):
    return jnp.sum((positions[:, None] >= doc_ends[None, :]).astype(jnp.int32), axis=1)


def matmul(left, right):
    return jnp.einsum("hij,hjk->hik", left, right, precision=HIGHEST)


def times_transposed(left, right):
    return jnp.einsum("hij,hkj->hik", left, right, precision=HIGHEST)


def block_pass(state_in, queries, keys_norm, values, intensity, doc_ids, prev_docs):
    head_count, length, head_depth = keys_norm.shape
    value_width = values.shape[2]
    blocks = prev_docs.shape[0]
    block_size = length // blocks
    query_blocks = queries.reshape(head_count, blocks, block_size, head_depth)
    key_blocks = keys_norm.reshape(head_count, blocks, block_size, head_depth)
    value_blocks = values.reshape(head_count, blocks, block_size, value_width)
    strength_blocks = intensity.reshape(head_count, blocks, block_size)
    block_ids = doc_ids.reshape(blocks, block_size)
    same_doc = (block_ids[:, :, None] == block_ids[:, None, :]).astype(jnp.float32)
    carried = (block_ids == prev_docs[:, None]).astype(jnp.float32)
    ones_table = jnp.ones((block_size, block_size), jnp.float32)
    strict_lower = jnp.tril(ones_table, -1)
    causal = jnp.tril(ones_table, 0)
    identity = jnp.eye(block_size, dtype=jnp.float32)
    key_gram = jnp.einsum("hncd,hned->hnce", key_blocks, key_blocks, precision=HIGHEST)
    system = identity + strength_blocks[..., :, None] * key_gram * same_doc[None] * strict_lower
    diagonal = identity * strength_blocks[..., :, None]
    solved = lax.linalg.triangular_solve(system, diagonal, left_side=True, lower=True)
    scores = (
        jnp.einsum("hncd,hned->hnce", query_blocks, key_blocks, precision=HIGHEST)
        * (same_doc * causal)[None]
    )
    last_doc = same_doc[:, -1, :]
    keep_state = carried[:, -1]

    def advance(carried_state, inputs):
        solved_b, scores_b, query_b, key_b, value_b, carried_b, last_b, keep_b = inputs
        projected = jnp.einsum("hcd,hvd->hcv", key_b, carried_state, precision=HIGHEST)
        deltas = jnp.einsum(
            "hts,hsv->htv",
            solved_b,
            value_b - carried_b[None, :, None] * projected,
            precision=HIGHEST,
        )
        outputs = carried_b[None, :, None] * jnp.einsum(
            "hcd,hvd->hcv", query_b, carried_state, precision=HIGHEST
        )
        outputs = outputs + jnp.einsum("hts,hsv->htv", scores_b, deltas, precision=HIGHEST)
        new_state = keep_b * carried_state + jnp.einsum(
            "hsv,hsd->hvd", deltas * last_b[None, :, None], key_b, precision=HIGHEST
        )
        return (new_state, outputs)

    inputs = (
        jnp.moveaxis(solved, 1, 0),
        jnp.moveaxis(scores, 1, 0),
        jnp.moveaxis(query_blocks, 1, 0),
        jnp.moveaxis(key_blocks, 1, 0),
        jnp.moveaxis(value_blocks, 1, 0),
        carried,
        last_doc,
        keep_state,
    )
    final_state, block_outs = lax.scan(advance, state_in, inputs)
    block_outs = jnp.moveaxis(block_outs, 0, 1).reshape(head_count, length, value_width)
    return (block_outs, final_state)


def butterfly(transfer, offset, adjoint_seed, identity, zero_state, shard_index, devices):
    totals = (transfer, offset, adjoint_seed)
    prefix = (identity, zero_state)
    suffix = (identity, zero_state)
    for bit_level in range(devices.bit_length() - 1):
        partner = from_partner(totals, "seq", bit_level)
        is_upper = shard_index // 2**bit_level % 2

        def from_lower(operand):
            new_prefix = (matmul(partner[0], prefix[0]), matmul(partner[1], prefix[0]) + prefix[1])
            new_totals = (
                matmul(partner[0], totals[0]),
                matmul(partner[1], totals[0]) + totals[1],
                times_transposed(totals[2], partner[0]) + partner[2],
            )
            return (new_prefix, suffix, new_totals)

        def from_upper(operand):
            new_suffix = (
                matmul(suffix[0], partner[0]),
                times_transposed(partner[2], suffix[0]) + suffix[1],
            )
            new_totals = (
                matmul(totals[0], partner[0]),
                matmul(totals[1], partner[0]) + partner[1],
                times_transposed(partner[2], totals[0]) + totals[2],
            )
            return (prefix, new_suffix, new_totals)

        prefix, suffix, totals = lax.cond(is_upper == 1, from_lower, from_upper, 0)
    return (prefix[1], suffix[1])


def shards_by_tokens(query_acts, key_acts, value_acts, beta_logit, output_grad, doc_lengths):
    devices = lax.axis_size("seq")
    shard_index = lax.axis_index("seq")
    length = query_acts.shape[0]
    head_count = beta_logit.shape[0]
    feature_width = query_acts.shape[1]
    head_depth = feature_width // head_count
    blocks = length // BLOCK
    gathered = lax.all_to_all(output_grad, "seq", split_axis=1, concat_axis=0, tiled=True)
    cotangent = (
        gathered.astype(jnp.float32).reshape(head_count, head_depth, length).transpose(0, 2, 1)
    )
    doc_ends = jnp.cumsum(doc_lengths)
    first_token = shard_index * length
    positions = first_token + jnp.arange(length, dtype=jnp.int32)
    doc_ids = count_ends(positions, doc_ends)
    starts = first_token + jnp.arange(blocks, dtype=jnp.int32) * BLOCK - 1
    prev_docs = jnp.where(starts >= 0, count_ends(starts, doc_ends), -1)

    def split_heads(values):
        return values.reshape(length, head_count, head_depth).transpose(1, 0, 2)

    query_f = query_acts.astype(jnp.float32)
    key_f = key_acts.astype(jnp.float32)
    value_f = value_acts.astype(jnp.float32)
    query_norm = normalize(split_heads(query_f))
    key_norm = normalize(split_heads(key_f))
    value_heads = split_heads(value_f)
    intensity = jax.nn.sigmoid(beta_logit)
    identity = jnp.broadcast_to(
        jnp.eye(head_depth, dtype=jnp.float32), (head_count, head_depth, head_depth)
    )
    zero_state = jnp.zeros((head_count, head_depth, head_depth), jnp.float32)
    lifted_state = jnp.concatenate([identity, zero_state], axis=1)
    lifted_values = jnp.concatenate([jnp.zeros_like(value_heads), value_heads], axis=2)
    lifted_out, lifted_end = block_pass(
        lifted_state, query_norm, key_norm, lifted_values, intensity, doc_ids, prev_docs
    )
    transfer = lifted_end[:, :head_depth]
    offset = lifted_end[:, head_depth:]
    response = lifted_out[..., :head_depth]
    adjoint_seed = jnp.einsum("htv,htd->hvd", cotangent, response, precision=HIGHEST)
    state_in, grad_out = butterfly(
        transfer, offset, adjoint_seed, identity, zero_state, shard_index, devices
    )

    def forward(query_in, key_in, value_in, logit_in):
        return block_pass(
            state_in,
            normalize(split_heads(query_in)),
            normalize(split_heads(key_in)),
            split_heads(value_in),
            jax.nn.sigmoid(logit_in),
            doc_ids,
            prev_docs,
        )

    pullback = jax.vjp(forward, query_f, key_f, value_f, beta_logit)[1]
    grads = pullback((cotangent, grad_out))
    query_local = grads[0].T.astype(jnp.bfloat16)
    query_grad = lax.all_to_all(query_local, "seq", split_axis=0, concat_axis=1, tiled=True)
    return (query_grad, grads[1].astype(jnp.bfloat16), grads[2].astype(jnp.bfloat16), grads[3])


def shards(query_acts, key_acts, value_acts, beta_logit, output_grad, doc_lengths):
    devices = lax.axis_size("seq")
    length, width = query_acts.shape
    head_count = beta_logit.shape[0]
    by_heads = devices == head_count and width == head_count * CHUNK and length == CHUNK
    if not by_heads or devices % GROUP or devices < 8:
        return shards_by_tokens(
            query_acts, key_acts, value_acts, beta_logit, output_grad, doc_lengths
        )
    logit = beta_logit.reshape(head_count, 1, length)
    query_grad, key_grad, value_grad, logit_grad = head_pass(
        query_acts, key_acts, value_acts, logit, output_grad, doc_lengths
    )
    return query_grad, key_grad, value_grad, logit_grad.reshape(head_count, length)


def solution(mesh):
    placed = (
        P(("groups", "seq"), None),
        P(("groups", "seq"), None),
        P(("groups", "seq"), None),
        P(None, ("groups", "seq")),
        P("seq", "groups"),
        P("groups"),
    )
    return jax.shard_map(
        shards,
        mesh=mesh,
        in_specs=placed,
        out_specs=(
            P("seq", "groups"),
            P(("groups", "seq"), None),
            P(("groups", "seq"), None),
            P(None, ("groups", "seq")),
        ),
        check_vma=False,
    )
```

```python
import functools
import jax
import jax.numpy as jnp
from jax import lax
from jax.experimental import pallas as pl
from jax.experimental.pallas import tpu as pltpu
from jax.sharding import PartitionSpec as P

BLOCK = 64
CHUNK = 128
GROUP = 4
LATE = 2
F32 = jnp.float32
BF16 = jnp.bfloat16


def dot(left, right, dims):
    return lax.dot_general(left, right, ((dims[:1], dims[1:]), ((), ())), preferred_element_type=F32)


def split(values):
    high = values.astype(BF16)
    return high, (values - high.astype(F32)).astype(BF16)


def dot2l(left, exact, dims=(1, 0)):
    high, low = left
    return dot(high, exact, dims) + dot(low, exact, dims)


def dot2r(exact, right, dims=(1, 0)):
    high, low = right
    return dot(exact, high, dims) + dot(exact, low, dims)


def dot3(left, right, dims=(1, 0)):
    return dot(left[0], right[0], dims) + (dot(left[1], right[0], dims) + dot(left[0], right[1], dims))


def across(column):
    return jnp.broadcast_to(column, (CHUNK, CHUNK)).T


def inverse_norm(values):
    wide = values.astype(F32)
    return lax.rsqrt(jnp.sum(wide * wide, axis=1, keepdims=True) + 1e-06)


def doc_of(positions, ends):
    total = jnp.zeros(jnp.shape(positions), jnp.int32)
    for end in ends:
        total = total + (positions >= end).astype(jnp.int32)
    return total


def chunk_masks(index, ends):
    first = index * CHUNK
    down = first + lax.broadcasted_iota(jnp.int32, (CHUNK, CHUNK), 0)
    over = first + lax.broadcasted_iota(jnp.int32, (CHUNK, CHUNK), 1)
    doc_down = doc_of(down, ends)
    doc_over = doc_of(over, ends)
    before = jnp.where(first > 0, doc_of(first - 1, ends), -1)
    last = doc_of(first + CHUNK - 1, ends)
    same = doc_down == doc_over
    causal = jnp.where(same & (down >= over), 1.0, 0.0)
    strict = jnp.where(same & (down > over), 1.0, 0.0)
    carried = jnp.where(doc_down == before, 1.0, 0.0)
    closing = jnp.where(doc_down == last, 1.0, 0.0)
    keep = jnp.where(before == last, 1.0, 0.0)
    return causal, strict, carried, closing, keep


def invert(systems):
    rows = lax.broadcasted_iota(jnp.int32, (CHUNK, CHUNK), 0)
    cols = lax.broadcasted_iota(jnp.int32, (CHUNK, CHUNK), 1)
    eye = jnp.where(rows == cols, 1.0, 0.0)
    size = 1
    solved = None
    while size < CHUNK:
        pair = (rows // (2 * size) == cols // (2 * size)) & (rows // size != cols // size)
        corners = [jnp.where(pair, system, 0.0) for system in systems]
        if solved is None:
            solved = [eye - corner for corner in corners]
        else:
            parts = [split(value) for value in solved]
            inner = [dot3(split(corner), part) for corner, part in zip(corners, parts)]
            solved = [
                value - dot3(part, split(middle))
                for value, part, middle in zip(solved, parts, inner)
            ]
        size *= 2
    return solved


def ends_of(lengths_ref):
    ends = []
    total = 0
    for i in range(lengths_ref.shape[0]):
        total = total + lengths_ref[i]
        ends.append(total)
    return ends


def prepare(indices, ends, load, store):
    items = []
    for index in indices:
        query, key, value, cotangent, strength = load(index)
        causal, strict, carried, closing, keep = chunk_masks(index, ends)
        norm_q, norm_k = inverse_norm(query), inverse_norm(key)
        key_over = across(norm_k)
        gram = dot(key, key, (1, 1)) * norm_k * key_over
        scores = dot(query, key, (1, 1)) * norm_q * key_over * causal
        strength_down = strength.T
        items.append(
            (index, query, key, value, cotangent, carried, closing, keep, norm_q, norm_k,
             key_over, scores, strength, strength_down * gram * strict)
        )
    solved = invert([item[-1] for item in items])
    for item, inverse in zip(items, solved):
        (index, query, key, value, cotangent, carried, closing, keep, norm_q, norm_k,
         key_over, scores, strength, _) = item
        weighted = inverse * strength
        local = dot2l(split(weighted), value)
        response_k = dot2l(split(weighted * key_over * carried.T), key)
        ending = dot2l(split((weighted * (closing * norm_k)).T), key)
        offset = dot2r(value, split(ending), (0, 0))
        step = dot2r(key, split(ending * (carried * norm_k)), (0, 0))
        scores_parts = split(scores)
        response = carried * norm_q * query.astype(F32) - dot3(scores_parts, split(response_k))
        seed = dot2r(cotangent, split(response))
        early = dot2l(split(scores.T), cotangent, (1, 1))
        store(index, inverse, scores, local, response_k, offset, step, seed, early)


def finish(index, ends, load, stored, state, adjoint):
    query, key, value, cotangent, strength = load(index)
    inverse, scores, local, response_k, early = stored
    causal, strict, carried, closing, keep = chunk_masks(index, ends)
    norm_q, norm_k = inverse_norm(query), inverse_norm(key)
    key_f = key.astype(F32) * norm_k
    query_f = query.astype(F32) * norm_q
    key_over = across(norm_k)
    query_over = across(norm_q)
    strength_down = strength.T
    state_parts = split(state)
    adjoint_parts = split(adjoint)
    turned = cotangent.astype(F32).T.astype(BF16)
    deltas = local - dot3(split(response_k), state_parts, (1, 1))
    delta_parts = split(deltas)
    delta_grad = early + closing * norm_k * dot2r(key, adjoint_parts, (1, 1))
    right_grad = dot3(split(inverse.T), split(delta_grad))
    value_grad = strength_down * right_grad
    logit_grad = (1.0 - strength_down) * jnp.sum(right_grad * deltas, axis=1, keepdims=True)
    system_grad = -strength_down * strict * dot3(split(right_grad), delta_parts, (1, 1))
    scores_grad = causal * dot2r(turned, delta_parts, (1, 1))
    gram_grad = system_grad + system_grad.T
    query_norm_grad = dot2l(split(scores_grad * key_over), key)
    query_norm_grad = query_norm_grad + carried * dot2r(turned, state_parts)
    key_norm_grad = dot2l(split(gram_grad * key_over), key)
    key_norm_grad = key_norm_grad + dot2l(split(scores_grad.T * query_over), query)
    key_norm_grad = key_norm_grad + dot3(split(closing * deltas), adjoint_parts)
    key_norm_grad = key_norm_grad - dot3(split(carried * value_grad), state_parts)
    query_grad = norm_q * (
        query_norm_grad - query_f * jnp.sum(query_f * query_norm_grad, axis=1, keepdims=True)
    )
    key_grad = norm_k * (
        key_norm_grad - key_f * jnp.sum(key_f * key_norm_grad, axis=1, keepdims=True)
    )
    return query_grad.T.astype(BF16), key_grad.astype(BF16), value_grad.astype(BF16), across(logit_grad)[:1]


def head_kernel(
    lengths_ref, query_ref, key_ref, value_ref, logit_ref, cotangent_ref,
    query_out, key_out, value_out, logit_out,
    query_in, key_in, value_in, logit_in, key_back, value_back, logit_back,
    inverse_ref, scores_ref, local_ref, response_ref, offset_ref, step_ref, seed_ref, early_ref,
    state_ref, adjoint_ref, turned_ref, turned_sem, in_send, in_recv, out_send, out_recv,
):
    chunks = key_in.shape[0]
    me = lax.axis_index("seq")
    ends = ends_of(lengths_ref)

    def columns(index):
        return pl.ds(pl.multiple_of(index * CHUNK, CHUNK), CHUNK)

    def ahead(offset):
        return lax.rem(me + offset, chunks)

    def in_pairs(owner, source):
        return [
            (key_ref.at[:, columns(owner)], key_in.at[source]),
            (value_ref.at[:, columns(owner)], value_in.at[source]),
            (query_ref.at[:, columns(owner)], query_in.at[source]),
            (logit_ref.at[owner], logit_in.at[source]),
        ]

    def out_pairs(index, head):
        return [
            (key_back.at[index], key_out.at[:, columns(head)]),
            (value_back.at[index], value_out.at[:, columns(head)]),
            (logit_back.at[index], logit_out.at[head]),
        ]

    def remote(pairs, send, recv, send_at, recv_at, peer):
        return [
            pltpu.make_async_remote_copy(
                src_ref=pair[0],
                dst_ref=pair[1],
                send_sem=send.at[i, send_at],
                recv_sem=recv.at[i, recv_at],
                device_id={"seq": peer},
                device_id_type=pl.DeviceIdType.MESH,
            )
            for i, pair in enumerate(pairs)
        ]

    def local_copies(pairs, sems):
        return [
            pltpu.make_async_copy(pair[0], pair[1], sems.at[i, me])
            for i, pair in enumerate(pairs)
        ]

    barrier = pltpu.get_barrier_semaphore()

    def greet(offset, carry):
        pl.semaphore_signal(
            barrier, inc=1, device_id={"seq": ahead(offset)}, device_id_type=pl.DeviceIdType.MESH
        )
        return carry

    own = local_copies(in_pairs(me, me), in_recv)
    for copy in own:
        copy.start()
    turned = pltpu.make_async_copy(cotangent_ref, turned_ref, turned_sem)
    turned.start()
    lax.fori_loop(1, chunks, greet, 0)
    pl.semaphore_wait(barrier, chunks - 1)

    def send(offset, carry):
        peer = ahead(offset)
        for copy in remote(in_pairs(peer, me), in_send, in_recv, peer, me, peer):
            copy.start()
        return carry

    lax.fori_loop(1, chunks, send, 0)
    for copy in own:
        copy.wait()
    turned.wait()

    def load(index):
        logit = jnp.broadcast_to(logit_in[index], (CHUNK, CHUNK))
        strength = 1.0 / (1.0 + jnp.exp(-logit))
        return (query_in[index], key_in[index], value_in[index],
                turned_ref[:, columns(index)], strength)

    def store(index, inverse, scores, local, response_k, offset, step, seed, early):
        inverse_ref[index] = inverse
        scores_ref[index] = scores
        local_ref[index] = local
        response_ref[index] = response_k
        offset_ref[index] = offset
        step_ref[index] = step
        seed_ref[index] = seed
        early_ref[index] = early

    def arrive(source):
        for copy in remote(in_pairs(me, source), in_send, in_recv, source, source, source):
            copy.wait_recv()

    def early_body(turn, carry):
        sources = [ahead(chunks - turn * GROUP - i) for i in range(GROUP)]

        @pl.when(turn > 0)
        def _():
            arrive(sources[0])

        for source in sources[1:]:
            arrive(source)
        prepare(sources, ends, load, store)
        return carry

    lax.fori_loop(0, chunks // GROUP, early_body, 0)

    def keep_of(index):
        first = index * CHUNK
        before = jnp.where(first > 0, doc_of(first - 1, ends), -1)
        return jnp.where(before == doc_of(first + CHUNK - 1, ends), 1.0, 0.0)

    def chain(turn, carry):
        state, adjoint = carry
        back = chunks - 1 - turn
        state_ref[turn] = state
        adjoint_ref[back] = adjoint
        moved = dot3(split(state), split(step_ref[turn]))
        pulled = dot3(split(adjoint), split(step_ref[back]), (1, 1))
        state = keep_of(turn) * state - moved + offset_ref[turn]
        adjoint = keep_of(back) * adjoint - pulled + seed_ref[back]
        return state, adjoint

    zero = jnp.zeros((CHUNK, CHUNK), F32)
    lax.fori_loop(0, chunks, chain, (zero, zero))

    def late_body(turn, carry):
        indices = [ahead(4 + turn * LATE + i) for i in range(LATE)]
        for index in indices:
            stored = (inverse_ref[index], scores_ref[index], local_ref[index],
                      response_ref[index], early_ref[index])
            results = finish(index, ends, load, stored, state_ref[index], adjoint_ref[index])
            query_out[:, columns(index)] = results[0]
            key_back[index] = results[1]
            value_back[index] = results[2]
            logit_back[index] = results[3]

        @pl.when(turn != (chunks - 4) // LATE)
        def _():
            for copy in remote(
                out_pairs(indices[0], me), out_send, out_recv, indices[0], me, indices[0]
            ):
                copy.start()

        @pl.when(turn == (chunks - 4) // LATE)
        def _():
            for copy in local_copies(out_pairs(me, me), out_recv):
                copy.start()

        for index in indices[1:]:
            for copy in remote(out_pairs(index, me), out_send, out_recv, index, me, index):
                copy.start()
        return carry

    lax.fori_loop(0, chunks // LATE, late_body, 0)

    for copy in local_copies(out_pairs(me, me), out_recv):
        copy.wait()

    def settle(offset, carry):
        peer = ahead(offset)
        for copy in remote(in_pairs(peer, me), in_send, in_recv, peer, me, peer):
            copy.wait_send()
        for copy in remote(out_pairs(peer, me), out_send, out_recv, peer, me, peer):
            copy.wait_send()
        for copy in remote(out_pairs(me, peer), out_send, out_recv, peer, peer, peer):
            copy.wait_recv()
        return carry

    lax.fori_loop(1, chunks, settle, 0)


def head_pass(query, key, value, logit, cotangent, lengths):
    length, width = query.shape
    heads = logit.shape[0]
    blocks = (heads, CHUNK, CHUNK)
    rows = (heads, 1, CHUNK)
    whole = pl.BlockSpec(memory_space=pltpu.VMEM)
    anywhere = pl.BlockSpec(memory_space=pl.ANY)
    return pl.pallas_call(
        head_kernel,
        in_specs=[pl.BlockSpec(memory_space=pltpu.SMEM), anywhere, anywhere, anywhere, anywhere, anywhere],
        out_specs=[whole, anywhere, anywhere, whole],
        out_shape=[
            jax.ShapeDtypeStruct((CHUNK, width), BF16),
            jax.ShapeDtypeStruct((length, width), BF16),
            jax.ShapeDtypeStruct((length, width), BF16),
            jax.ShapeDtypeStruct(rows, F32),
        ],
        scratch_shapes=[pltpu.VMEM(blocks, BF16)] * 3
        + [pltpu.VMEM(rows, F32)]
        + [pltpu.VMEM(blocks, BF16)] * 2
        + [pltpu.VMEM(rows, F32)]
        + [pltpu.VMEM(blocks, F32)] * 10
        + [pltpu.VMEM((CHUNK, width), BF16), pltpu.SemaphoreType.DMA]
        + [pltpu.SemaphoreType.DMA((4, heads))] * 2
        + [pltpu.SemaphoreType.DMA((3, heads))] * 2,
        compiler_params=pltpu.CompilerParams(
            vmem_limit_bytes=63 << 20, collective_id=0, has_side_effects=True
        ),
    )(lengths, query, key, value, logit, cotangent)


HIGHEST = lax.Precision.HIGHEST


def from_partner(block, axis, bit):
    count = lax.axis_size(axis)
    route = []
    for low in range(count):
        high = low | 1 << bit
        if high != low and high < count:
            route += [(low, high), (high, low)]
    return lax.ppermute(block, axis, route)


def normalize(values):
    return values * lax.rsqrt(jnp.sum(values * values, axis=-1, keepdims=True) + 1e-06)


def count_ends(positions, doc_ends):
    return jnp.sum((positions[:, None] >= doc_ends[None, :]).astype(jnp.int32), axis=1)


def matmul(left, right):
    return jnp.einsum("hij,hjk->hik", left, right, precision=HIGHEST)


def times_transposed(left, right):
    return jnp.einsum("hij,hkj->hik", left, right, precision=HIGHEST)


def block_pass(state_in, queries, keys_norm, values, intensity, doc_ids, prev_docs):
    head_count, length, head_depth = keys_norm.shape
    value_width = values.shape[2]
    blocks = prev_docs.shape[0]
    block_size = length // blocks
    query_blocks = queries.reshape(head_count, blocks, block_size, head_depth)
    key_blocks = keys_norm.reshape(head_count, blocks, block_size, head_depth)
    value_blocks = values.reshape(head_count, blocks, block_size, value_width)
    strength_blocks = intensity.reshape(head_count, blocks, block_size)
    block_ids = doc_ids.reshape(blocks, block_size)
    same_doc = (block_ids[:, :, None] == block_ids[:, None, :]).astype(jnp.float32)
    carried = (block_ids == prev_docs[:, None]).astype(jnp.float32)
    ones_table = jnp.ones((block_size, block_size), jnp.float32)
    strict_lower = jnp.tril(ones_table, -1)
    causal = jnp.tril(ones_table, 0)
    identity = jnp.eye(block_size, dtype=jnp.float32)
    key_gram = jnp.einsum("hncd,hned->hnce", key_blocks, key_blocks, precision=HIGHEST)
    system = identity + strength_blocks[..., :, None] * key_gram * same_doc[None] * strict_lower
    diagonal = identity * strength_blocks[..., :, None]
    solved = lax.linalg.triangular_solve(system, diagonal, left_side=True, lower=True)
    scores = (
        jnp.einsum("hncd,hned->hnce", query_blocks, key_blocks, precision=HIGHEST)
        * (same_doc * causal)[None]
    )
    last_doc = same_doc[:, -1, :]
    keep_state = carried[:, -1]

    def advance(carried_state, inputs):
        solved_b, scores_b, query_b, key_b, value_b, carried_b, last_b, keep_b = inputs
        projected = jnp.einsum("hcd,hvd->hcv", key_b, carried_state, precision=HIGHEST)
        deltas = jnp.einsum(
            "hts,hsv->htv",
            solved_b,
            value_b - carried_b[None, :, None] * projected,
            precision=HIGHEST,
        )
        outputs = carried_b[None, :, None] * jnp.einsum(
            "hcd,hvd->hcv", query_b, carried_state, precision=HIGHEST
        )
        outputs = outputs + jnp.einsum("hts,hsv->htv", scores_b, deltas, precision=HIGHEST)
        new_state = keep_b * carried_state + jnp.einsum(
            "hsv,hsd->hvd", deltas * last_b[None, :, None], key_b, precision=HIGHEST
        )
        return (new_state, outputs)

    inputs = (
        jnp.moveaxis(solved, 1, 0),
        jnp.moveaxis(scores, 1, 0),
        jnp.moveaxis(query_blocks, 1, 0),
        jnp.moveaxis(key_blocks, 1, 0),
        jnp.moveaxis(value_blocks, 1, 0),
        carried,
        last_doc,
        keep_state,
    )
    final_state, block_outs = lax.scan(advance, state_in, inputs)
    block_outs = jnp.moveaxis(block_outs, 0, 1).reshape(head_count, length, value_width)
    return (block_outs, final_state)


def butterfly(transfer, offset, adjoint_seed, identity, zero_state, shard_index, devices):
    totals = (transfer, offset, adjoint_seed)
    prefix = (identity, zero_state)
    suffix = (identity, zero_state)
    for bit_level in range(devices.bit_length() - 1):
        partner = from_partner(totals, "seq", bit_level)
        is_upper = shard_index // 2**bit_level % 2

        def from_lower(operand):
            new_prefix = (matmul(partner[0], prefix[0]), matmul(partner[1], prefix[0]) + prefix[1])
            new_totals = (
                matmul(partner[0], totals[0]),
                matmul(partner[1], totals[0]) + totals[1],
                times_transposed(totals[2], partner[0]) + partner[2],
            )
            return (new_prefix, suffix, new_totals)

        def from_upper(operand):
            new_suffix = (
                matmul(suffix[0], partner[0]),
                times_transposed(partner[2], suffix[0]) + suffix[1],
            )
            new_totals = (
                matmul(totals[0], partner[0]),
                matmul(totals[1], partner[0]) + partner[1],
                times_transposed(partner[2], totals[0]) + totals[2],
            )
            return (prefix, new_suffix, new_totals)

        prefix, suffix, totals = lax.cond(is_upper == 1, from_lower, from_upper, 0)
    return (prefix[1], suffix[1])


def shards_by_tokens(query_acts, key_acts, value_acts, beta_logit, output_grad, doc_lengths):
    devices = lax.axis_size("seq")
    shard_index = lax.axis_index("seq")
    length = query_acts.shape[0]
    head_count = beta_logit.shape[0]
    feature_width = query_acts.shape[1]
    head_depth = feature_width // head_count
    blocks = length // BLOCK
    gathered = lax.all_to_all(output_grad, "seq", split_axis=1, concat_axis=0, tiled=True)
    cotangent = (
        gathered.astype(jnp.float32).reshape(head_count, head_depth, length).transpose(0, 2, 1)
    )
    doc_ends = jnp.cumsum(doc_lengths)
    first_token = shard_index * length
    positions = first_token + jnp.arange(length, dtype=jnp.int32)
    doc_ids = count_ends(positions, doc_ends)
    starts = first_token + jnp.arange(blocks, dtype=jnp.int32) * BLOCK - 1
    prev_docs = jnp.where(starts >= 0, count_ends(starts, doc_ends), -1)

    def split_heads(values):
        return values.reshape(length, head_count, head_depth).transpose(1, 0, 2)

    query_f = query_acts.astype(jnp.float32)
    key_f = key_acts.astype(jnp.float32)
    value_f = value_acts.astype(jnp.float32)
    query_norm = normalize(split_heads(query_f))
    key_norm = normalize(split_heads(key_f))
    value_heads = split_heads(value_f)
    intensity = jax.nn.sigmoid(beta_logit)
    identity = jnp.broadcast_to(
        jnp.eye(head_depth, dtype=jnp.float32), (head_count, head_depth, head_depth)
    )
    zero_state = jnp.zeros((head_count, head_depth, head_depth), jnp.float32)
    lifted_state = jnp.concatenate([identity, zero_state], axis=1)
    lifted_values = jnp.concatenate([jnp.zeros_like(value_heads), value_heads], axis=2)
    lifted_out, lifted_end = block_pass(
        lifted_state, query_norm, key_norm, lifted_values, intensity, doc_ids, prev_docs
    )
    transfer = lifted_end[:, :head_depth]
    offset = lifted_end[:, head_depth:]
    response = lifted_out[..., :head_depth]
    adjoint_seed = jnp.einsum("htv,htd->hvd", cotangent, response, precision=HIGHEST)
    state_in, grad_out = butterfly(
        transfer, offset, adjoint_seed, identity, zero_state, shard_index, devices
    )

    def forward(query_in, key_in, value_in, logit_in):
        return block_pass(
            state_in,
            normalize(split_heads(query_in)),
            normalize(split_heads(key_in)),
            split_heads(value_in),
            jax.nn.sigmoid(logit_in),
            doc_ids,
            prev_docs,
        )

    pullback = jax.vjp(forward, query_f, key_f, value_f, beta_logit)[1]
    grads = pullback((cotangent, grad_out))
    query_local = grads[0].T.astype(jnp.bfloat16)
    query_grad = lax.all_to_all(query_local, "seq", split_axis=0, concat_axis=1, tiled=True)
    return (query_grad, grads[1].astype(jnp.bfloat16), grads[2].astype(jnp.bfloat16), grads[3])


def shards(query_acts, key_acts, value_acts, beta_logit, output_grad, doc_lengths):
    devices = lax.axis_size("seq")
    length, width = query_acts.shape
    head_count = beta_logit.shape[0]
    by_heads = devices == head_count and width == head_count * CHUNK and length == CHUNK
    if not by_heads or devices % GROUP or devices < 8:
        return shards_by_tokens(
            query_acts, key_acts, value_acts, beta_logit, output_grad, doc_lengths
        )
    logit = beta_logit.reshape(head_count, 1, length)
    query_grad, key_grad, value_grad, logit_grad = head_pass(
        query_acts, key_acts, value_acts, logit, output_grad, doc_lengths
    )
    return query_grad, key_grad, value_grad, logit_grad.reshape(head_count, length)


def solution(mesh):
    placed = (
        P(("groups", "seq"), None),
        P(("groups", "seq"), None),
        P(("groups", "seq"), None),
        P(None, ("groups", "seq")),
        P("seq", "groups"),
        P("groups"),
    )
    return jax.shard_map(
        shards,
        mesh=mesh,
        in_specs=placed,
        out_specs=(
            P("seq", "groups"),
            P(("groups", "seq"), None),
            P(("groups", "seq"), None),
            P(None, ("groups", "seq")),
        ),
        check_vma=False,
    )
```
